256 devices in a mesh: redist: 128 (over y, z, x), rep: 2 (over core).
Axes of the slice: x: 4, y: 4, z: 8, core: 2. Of those that a mesh axis runs over, the one named last changes fastest.
Arguments:
- amplitudes: float32 [8, 256, 2, 3840], P(None, 'redist', 'rep'), may hold values from -6 to 6
- integrals: float32 [128, 1920, 2, 960], P('redist', None, 'rep'), may hold values from -0.0625 to 0.0625
- pair_count: int32 [8], replicated, may hold values from 5760 to 7680, as said below
Outputs:
- cycle_term: float32 [8, 256, 2, 3840], P(None, 'redist', 'rep')
The draws below stay inside these ranges and needn't reach their ends.
Inputs may be any that keep to these rules, and one draw needn't show every extreme that they name: `pair_count`: each block has at least 5760 live pair slots; some block has all 7680 live.
All inputs are finite; a program needn't handle non-finite values.
Results may differ from the reference program's by a relative error of at most 0.00007.
Values sent between devices are 32-bit elements; how exact they have to be, the bound alone decides.
No kernel may reach another device: no remote copies, remote signals or barrier semaphores. Data moves between devices by JAX's collectives and lax.ppermute only.
A program may use at most 64 MiB of HBM per device.

```python
import jax
import jax.numpy as jnp
from jax import lax

NBLK = 8
HP = 3840
RB = 256
PCAP = 7680
KSPLIT = 4
JSPLIT = 4
JW = 1920
KW = 960


def draw_pair_count(key, part):
    key_base, key_pick = jax.random.split(jax.random.fold_in(key, 17))
    count_base = jax.random.randint(key_base, (NBLK,), PCAP * 3 // 4, PCAP + 1)
    chosen = jax.random.randint(key_pick, (), 0, NBLK)
    return jnp.where(lax.iota(jnp.int32, NBLK) == chosen, PCAP, count_base).astype(jnp.int32)


def levels(own_key, shape, shards, least, largest):
    factor_of = 1.0
    for position, shards_of in shards:
        steps = jax.random.uniform(jax.random.fold_in(jax.random.fold_in(own_key, 6), position), (shards_of,), jnp.float32, least / len(shards), largest / len(shards))
        factor_of = factor_of * jnp.repeat(jnp.exp(steps), shape[position] // shards_of).reshape((-1,) + (1,) * (len(shape) - 1 - position))
    return factor_of


def normal_values(rng, dims, scale, reach, shards=(), kind=jnp.bfloat16):
    level = levels(rng, dims, shards, -0.22, 0.18) if shards else 1.0
    entries = jax.random.normal(rng, dims, jnp.float32) * scale * level
    return jnp.minimum(jnp.maximum(entries, -reach), reach).astype(kind)


def setup_inputs(seed: int = 0) -> dict:
    seeds = jax.random.split(jax.random.key(seed), 4)
    amplitudes = normal_values(seeds[0], (NBLK, RB, 2, HP), 1.0, 6.0, ((1, 128), (2, 2)), jnp.float32)
    integrals = normal_values(seeds[1], (NBLK * JSPLIT * KSPLIT, JW, 2, KW), PCAP ** -0.5, 0.0625, ((0, 128), (2, 2)), jnp.float32)
    pair_count = draw_pair_count(jax.random.fold_in(seeds[3], 71), 0)
    return dict(amplitudes=amplitudes, integrals=integrals, pair_count=pair_count)


def reference(amplitudes, integrals, pair_count):
    pair_slots = 2 * HP
    slot_index = lax.iota(jnp.int32, pair_slots)
    live_mask = (slot_index[None, :] < pair_count[:, None]).astype(jnp.float32)
    masked_amp = amplitudes.reshape(NBLK, RB, pair_slots) * live_mask[:, None, :]
    tiles = integrals.reshape(NBLK, JSPLIT, KSPLIT, JW, 2, KW)

    def one_block(operands):
        block_amp, block_tiles, block_mask = operands
        weight = block_tiles.transpose(0, 2, 3, 1, 4).reshape(pair_slots, pair_slots)
        product = lax.dot_general(block_amp, weight, (((1,), (1,)), ((), ())), precision=lax.Precision.HIGHEST, preferred_element_type=jnp.float32)
        return product * block_mask[None, :]

    cycle_term = lax.map(one_block, (masked_amp, tiles, live_mask))
    return cycle_term.reshape(NBLK, RB, 2, HP)
```

```python
import jax
import jax.numpy as jnp
from jax import lax
from jax.sharding import Mesh, PartitionSpec as P

NBLK = 8
YZ = ("y", "zh", "zl")
YZX = ("y", "zh", "zl", "x")
SWAP = [(0, 1), (1, 0)]


def on_device(amplitudes, integrals, pair_count):
    half_slots = amplitudes.shape[3]
    rows = amplitudes.shape[1]
    col_width = integrals.shape[1]
    kc_width = integrals.shape[3]
    kc_split = half_slots // kc_width
    jb_split = 2 * half_slots // col_width
    owners = lax.axis_size("y") * lax.axis_size("zh") * lax.axis_size("zl")
    half = lax.axis_index("rep")
    first = half == 0
    slot_index = half * half_slots + lax.iota(jnp.int32, half_slots)
    live_mask = (slot_index[None, :] < pair_count[:, None]).astype(jnp.float32)
    masked = amplitudes[:, :, 0, :] * live_mask[:, None, :]
    pieces = masked.reshape(NBLK, rows, kc_split, kc_width).transpose(0, 2, 1, 3)
    outgoing = jnp.broadcast_to(
        pieces[:, None], (NBLK, jb_split, kc_split, rows, kc_width)
    ).reshape(-1, rows, kc_width)
    arrived = lax.all_to_all(outgoing, YZX, split_axis=0, concat_axis=0, tiled=True)
    tile = integrals[0, :, 0, :]
    partial = jnp.einsum(
        "srk,jk->srj",
        arrived,
        tile,
        precision=lax.Precision.HIGH,
        preferred_element_type=jnp.float32,
    )
    width = col_width // 2
    low, high = partial[:, :, :width], partial[:, :, width:]
    away = jnp.where(first, high, low)
    own = jnp.where(first, low, high)
    pair_sum = own + lax.ppermute(away, "rep", SWAP)
    by_x = pair_sum.reshape(owners, -1, rows, width).transpose(1, 0, 2, 3)
    gathered = lax.all_to_all(by_x, "x", split_axis=0, concat_axis=0, tiled=True)
    summed = gathered.sum(axis=0)
    moved = lax.all_to_all(summed, YZ, split_axis=0, concat_axis=0, tiled=True)
    by_half = moved.reshape(NBLK, 2, jb_split // 2, rows, width)
    mine = jnp.where(first, by_half[:, 0], by_half[:, 1])
    theirs = jnp.where(first, by_half[:, 1], by_half[:, 0])
    other = lax.ppermute(theirs, "rep", SWAP)
    low = jnp.where(first, mine, other)
    high = jnp.where(first, other, mine)
    both = jnp.stack([low, high], axis=2)
    result = both.transpose(0, 3, 1, 2, 4).reshape(NBLK, rows, half_slots)
    return (result * live_mask[:, None, :])[:, :, None, :]


def solution(mesh):
    fine = Mesh(
        mesh.devices.reshape(4, 2, 4, 4, 2), ("y", "zh", "zl", "x", "rep")
    )
    placed = (P(None, YZX, "rep", None), P(YZX, None, "rep", None), P())
    return jax.shard_map(
        on_device,
        mesh=fine,
        in_specs=placed,
        out_specs=P(None, YZX, "rep", None),
        check_vma=False,
    )
```

```python
import functools

import jax
import jax.numpy as jnp
from jax import lax
from jax.experimental import pallas as pl
from jax.experimental.pallas import tpu as pltpu
from jax.sharding import Mesh, PartitionSpec as P

NBLK = 8
YZX = ("y", "z", "x")
SWAP = [(0, 1), (1, 0)]
RING = 4
DEEP = 8
OWNERS = 32
LANES = 128
PART = 1024
STEP = 896
CHUNKS = 1
VMEM = pl.BlockSpec(memory_space=pltpu.VMEM)
SMEM = pl.BlockSpec(memory_space=pltpu.SMEM)
ANY = pl.BlockSpec(memory_space=pl.ANY)


def shift(value, axis, by):
    n = lax.axis_size(axis)
    return lax.ppermute(value, axis, [(i, (i + by) % n) for i in range(n)])


def pick(value, index, axis=0):
    return lax.dynamic_index_in_dim(value, index, axis, keepdims=False)


def params(mib):
    return pltpu.CompilerParams(vmem_limit_bytes=mib << 20)


def cost(flops, nbytes):
    return pl.CostEstimate(flops=flops, bytes_accessed=nbytes, transcendentals=0)


def live_limit(count_ref):
    return count_ref[lax.axis_index("y") * 2 + lax.axis_index("z") // RING]


def prepare_kernel(amp_ref, out_hbm, piece_ref, sems):
    width = piece_ref.shape[3]
    for g in range(NBLK):
        for r in range(2):
            row = amp_ref[g, r]
            for k in range(RING):
                piece_ref[g, k, r : r + 1, :] = row[:, k * width : (k + 1) * width]
    copies = [
        pltpu.make_async_copy(piece_ref, out_hbm.at[:, j], sems.at[j]) for j in range(RING)
    ]
    for copy in copies:
        copy.start()
    for copy in copies:
        copy.wait()


def prepare(amplitudes, width):
    return pl.pallas_call(
        prepare_kernel,
        in_specs=[VMEM],
        out_specs=ANY,
        out_shape=jax.ShapeDtypeStruct((NBLK, RING, RING, 2, width), jnp.float32),
        scratch_shapes=[
            pltpu.VMEM((NBLK, RING, 2, width), jnp.float32),
            pltpu.SemaphoreType.DMA((RING,)),
        ],
        cost_estimate=cost(0, 5 * 4 * amplitudes.size),
        compiler_params=params(56),
        name="prepare",
    )(amplitudes)


def arrange_kernel(count_ref, got_ref, out_ref):
    width = got_ref.shape[3]
    base = lax.axis_index("rep") * (RING * width) + lax.axis_index("x") * width
    slot = lax.broadcasted_iota(jnp.int32, (1, width), 1) + base
    live = (slot < live_limit(count_ref)).astype(jnp.float32)
    for x in range(RING):
        for r in range(2):
            at = (x * 2 + r) * OWNERS
            out_ref[at : at + OWNERS, :] = got_ref[:, x, r, :] * live


def arrange(pair_count, got):
    width = got.shape[3]
    rows = OWNERS * RING * 2
    return pl.pallas_call(
        arrange_kernel,
        in_specs=[SMEM, VMEM],
        out_specs=VMEM,
        out_shape=jax.ShapeDtypeStruct((rows, width), jnp.float32),
        cost_estimate=cost(0, 8 * rows * width),
        compiler_params=params(16),
        name="arrange",
    )(pair_count, got)


def gather_kernel(*refs):
    out_ref = refs[-1]
    width = PART // CHUNKS
    for c in range(CHUNKS):
        p = refs[c * RING : (c + 1) * RING]
        for r in range(2):
            at = slice(r * OWNERS, (r + 1) * OWNERS)
            total = (p[0][at] + p[1][at]) + (p[2][at] + p[3][at])
            out_ref[:, r, c * width : (c + 1) * width] = total


def gather(parts):
    return pl.pallas_call(
        gather_kernel,
        in_specs=[VMEM] * len(parts),
        out_specs=VMEM,
        out_shape=jax.ShapeDtypeStruct((OWNERS, 2, PART), jnp.float32),
        compiler_params=params(16),
        cost_estimate=cost(0, 5 * 4 * OWNERS * 2 * PART),
        name="gather_rows",
    )(*parts)


def final_kernel(moved_ref, other_ref, out_ref):
    def write(low_of, high_of):
        for g in range(NBLK):
            for r in range(2):
                for j in range(2):
                    base = j * (PART + STEP)
                    out_ref[g, r, :, base : base + PART] = low_of(g, j, r)
                    out_ref[g, r, :, base + PART : base + PART + STEP] = high_of(g, j, r)[:, LANES:]

    half = lax.axis_index("rep")

    @pl.when(half == 0)
    def _():
        write(
            lambda g, j, r: moved_ref[g, j, r : r + 1, :],
            lambda g, j, r: other_ref[g, j, r : r + 1, :],
        )

    @pl.when(half == 1)
    def _():
        write(
            lambda g, j, r: other_ref[g, j, r : r + 1, :],
            lambda g, j, r: moved_ref[g, 2 + j, r : r + 1, :],
        )


def final(moved, other, shape):
    return pl.pallas_call(
        final_kernel,
        in_specs=[VMEM, VMEM],
        out_specs=VMEM,
        out_shape=jax.ShapeDtypeStruct(shape, jnp.float32),
        compiler_params=params(16),
        name="final_rows",
    )(moved, other)


def contract(rows, integrals, pair_count):
    width = integrals.shape[1]
    limit = pick(pair_count, lax.axis_index("y") * 2 + lax.axis_index("z") // RING)
    column = (lax.axis_index("z") % RING) * width + lax.iota(jnp.int32, width)
    keep = (column < limit).astype(jnp.float32)
    partial = jnp.einsum(
        "rk,jk->rj",
        rows,
        integrals[0, :, 0, :],
        precision=lax.Precision.HIGH,
        preferred_element_type=jnp.float32,
    )
    partial = partial * keep[None, :]
    return partial[:, :PART], partial[:, STEP:]


def on_device(amplitudes, integrals, pair_count):
    kc_width = integrals.shape[3]
    half = lax.axis_index("rep")
    my_x = lax.axis_index("x")
    outgoing = prepare(amplitudes, kc_width).reshape(-1, 2, kc_width)
    got = lax.all_to_all(outgoing, YZX, split_axis=0, concat_axis=0, tiled=True)
    rows = arrange(pair_count, got.reshape(OWNERS, RING, 2, kc_width))
    low, high = contract(rows, integrals, pair_count)
    first = half == 0
    pair_sum = jnp.where(first, low, high) + lax.ppermute(jnp.where(first, high, low), "rep", SWAP)
    pair_sum = pair_sum.reshape(RING, 2 * OWNERS, PART)
    parts = [pick(pair_sum, my_x)]
    for s in range(1, RING):
        parts.append(shift(pick(pair_sum, (my_x + s) % RING), "x", s))
    leaving = gather(parts)
    moved = lax.all_to_all(leaving, ("y", "z"), split_axis=0, concat_axis=0, tiled=True)
    moved = moved.reshape(NBLK, RING, 2, PART)
    theirs = lax.dynamic_slice_in_dim(moved, (1 - half) * 2, 2, axis=1)
    other = lax.ppermute(theirs, "rep", SWAP)
    return final(moved, other, amplitudes.shape)


def solution(mesh):
    fine = Mesh(mesh.devices.reshape(4, 8, 4, 2), ("y", "z", "x", "rep"))
    placed = (P(None, YZX, "rep", None), P(YZX, None, "rep", None), P())
    return jax.shard_map(
        on_device,
        mesh=fine,
        in_specs=placed,
        out_specs=P(None, YZX, "rep", None),
        check_vma=False,
    )
```

```python
import functools

import jax
import jax.numpy as jnp
from jax import lax
from jax.experimental import pallas as pl
from jax.experimental.pallas import tpu as pltpu
from jax.sharding import Mesh, PartitionSpec as P

NBLK = 8
YZX = ("y", "z", "x")
SWAP = [(0, 1), (1, 0)]
RING = 4
DEEP = 8
OWNERS = 32
LANES = 128
PART = 1024
STEP = 896
SPLIT_MIB = 56
VMEM = pl.BlockSpec(memory_space=pltpu.VMEM)
SMEM = pl.BlockSpec(memory_space=pltpu.SMEM)
ANY = pl.BlockSpec(memory_space=pl.ANY)


def shift(value, axis, by):
    n = lax.axis_size(axis)
    return lax.ppermute(value, axis, [(i, (i + by) % n) for i in range(n)])


def pick(value, index, axis=0):
    return lax.dynamic_index_in_dim(value, index, axis, keepdims=False)


def params(mib):
    return pltpu.CompilerParams(vmem_limit_bytes=mib << 20)


def cost(flops, nbytes):
    return pl.CostEstimate(flops=flops, bytes_accessed=nbytes, transcendentals=0)


def live_limit(count_ref):
    return count_ref[lax.axis_index("y") * 2 + lax.axis_index("z") // RING]


def prepare_kernel(amp_ref, out_hbm, piece_ref, sems):
    width = piece_ref.shape[3]
    for g in range(NBLK):
        for r in range(2):
            row = amp_ref[g, r]
            for k in range(RING):
                piece_ref[g, k, r : r + 1, :] = row[:, k * width : (k + 1) * width]
    copies = [
        pltpu.make_async_copy(piece_ref, out_hbm.at[:, j], sems.at[j]) for j in range(RING)
    ]
    for copy in copies:
        copy.start()
    for copy in copies:
        copy.wait()


def prepare(amplitudes, width):
    return pl.pallas_call(
        prepare_kernel,
        in_specs=[VMEM],
        out_specs=ANY,
        out_shape=jax.ShapeDtypeStruct((NBLK, RING, RING, 2, width), jnp.float32),
        scratch_shapes=[
            pltpu.VMEM((NBLK, RING, 2, width), jnp.float32),
            pltpu.SemaphoreType.DMA((RING,)),
        ],
        cost_estimate=cost(0, 5 * 4 * amplitudes.size),
        compiler_params=params(56),
        name="prepare",
    )(amplitudes)


def split_kernel(count_ref, w_ref, *out_refs):
    half = lax.axis_index("rep")
    limit = live_limit(count_ref)
    base = (lax.axis_index("z") % RING) * w_ref.shape[1]
    for place, side in ((0, 1 - half), (1, half)):
        start = pl.multiple_of(side * STEP, LANES)
        high_ref, low_ref = out_refs[2 * place : 2 * place + 2]
        column = base + start + lax.broadcasted_iota(jnp.int32, (1, PART), 1)
        live = (column < limit).astype(jnp.float32)
        w = w_ref[:, pl.ds(start, PART)] * live
        high = w.astype(jnp.bfloat16)
        high_ref[...] = high
        low_ref[...] = (w - high.astype(jnp.float32)).astype(jnp.bfloat16)


def split_tile(pair_count, tile):
    depth, width = tile.shape
    rows = depth // 10
    return pl.pallas_call(
        split_kernel,
        grid=(10,),
        in_specs=[SMEM, pl.BlockSpec((rows, width), lambda i: (i, 0))],
        out_specs=[pl.BlockSpec((rows, PART), lambda i: (i, 0))] * 4,
        out_shape=[jax.ShapeDtypeStruct((depth, PART), jnp.bfloat16)] * 4,
        cost_estimate=cost(4 * depth * width, 8 * depth * width),
        compiler_params=params(SPLIT_MIB),
        name="split_tile",
    )(pair_count, tile)


def arrange_kernel(count_ref, got_ref, both_ref):
    width = got_ref.shape[3]
    rows = both_ref.shape[0] // 2
    base = lax.axis_index("rep") * (RING * width) + lax.axis_index("x") * width
    slot = lax.broadcasted_iota(jnp.int32, (1, width), 1) + base
    live = (slot < live_limit(count_ref)).astype(jnp.float32)
    for x in range(RING):
        for r in range(2):
            a = got_ref[:, x, r, :] * live
            high = a.astype(jnp.bfloat16)
            at = (x * 2 + r) * OWNERS
            both_ref[at : at + OWNERS, :] = high
            both_ref[rows + at : rows + at + OWNERS, :] = (a - high.astype(jnp.float32)).astype(
                jnp.bfloat16
            )


def arrange(pair_count, got):
    width = got.shape[3]
    rows = OWNERS * RING * 2
    return pl.pallas_call(
        arrange_kernel,
        in_specs=[SMEM, VMEM],
        out_specs=VMEM,
        out_shape=jax.ShapeDtypeStruct((2 * rows, width), jnp.bfloat16),
        cost_estimate=cost(0, 8 * rows * width),
        compiler_params=params(16),
        name="arrange",
    )(pair_count, got)


def contract(both, high, low):
    rows = both.shape[0] // 2
    dims = (((1,), (0,)), ((), ()))
    first = lax.dot_general(both, high, dims, preferred_element_type=jnp.float32)
    second = lax.dot_general(both[:rows], low, dims, preferred_element_type=jnp.float32)
    return first[:rows] + (first[rows:] + second)


def gather_kernel(own_ref, left_a, right_a, left_b, right_b, out_ref):
    out_ref[:, 0, :] = own_ref[:OWNERS] + (left_a[...] + right_a[...])
    out_ref[:, 1, :] = own_ref[OWNERS:] + (left_b[...] + right_b[...])


def gather(parts):
    return pl.pallas_call(
        gather_kernel,
        in_specs=[VMEM] * len(parts),
        out_specs=VMEM,
        out_shape=jax.ShapeDtypeStruct((OWNERS, 2, PART), jnp.float32),
        compiler_params=params(16),
        cost_estimate=cost(0, 4 * 4 * OWNERS * 2 * PART),
        name="gather_rows",
    )(*parts)


def final_kernel(moved_ref, other_ref, out_ref):
    def write(low_of, high_of):
        for g in range(NBLK):
            for r in range(2):
                for j in range(2):
                    base = j * (PART + STEP)
                    out_ref[g, r, :, base : base + PART] = low_of(g, j, r)
                    out_ref[g, r, :, base + PART : base + PART + STEP] = high_of(g, j, r)[:, LANES:]

    half = lax.axis_index("rep")

    @pl.when(half == 0)
    def _():
        write(
            lambda g, j, r: moved_ref[g, j, r : r + 1, :],
            lambda g, j, r: other_ref[g, j, r : r + 1, :],
        )

    @pl.when(half == 1)
    def _():
        write(
            lambda g, j, r: other_ref[g, j, r : r + 1, :],
            lambda g, j, r: moved_ref[g, 2 + j, r : r + 1, :],
        )


def final(moved, other, shape):
    return pl.pallas_call(
        final_kernel,
        in_specs=[VMEM, VMEM],
        out_specs=VMEM,
        out_shape=jax.ShapeDtypeStruct(shape, jnp.float32),
        compiler_params=params(16),
        name="final_rows",
    )(moved, other)


def on_device(amplitudes, integrals, pair_count):
    kc_width = integrals.shape[3]
    half = lax.axis_index("rep")
    my_x = lax.axis_index("x")
    outgoing = prepare(amplitudes, kc_width).reshape(-1, 2, kc_width)
    got = lax.all_to_all(outgoing, YZX, split_axis=0, concat_axis=0, tiled=True)
    split = split_tile(pair_count, integrals[0, :, 0, :].T)
    got, split = lax.optimization_barrier((got, split))
    both = arrange(pair_count, got.reshape(OWNERS, RING, 2, kc_width))
    arrived = lax.ppermute(contract(both, split[0], split[1]), "rep", SWAP)
    pair_sum = contract(both, split[2], split[3]) + arrived
    pair_sum = pair_sum.reshape(RING, 2, OWNERS, PART)
    ours, right, across, left = [pick(pair_sum, (my_x + s) % RING) for s in range(RING)]
    by_right = shift(across[0], "x", 1)
    by_left = shift(across[1], "x", -1)
    right_b = shift(right[1], "x", 1)
    left_a = shift(left[0], "x", -1)
    right_a = shift(right[0] + by_right, "x", 1)
    left_b = shift(left[1] + by_left, "x", -1)
    leaving = gather([ours.reshape(2 * OWNERS, PART), left_a, right_a, left_b, right_b])
    moved = lax.all_to_all(leaving, ("y", "z"), split_axis=0, concat_axis=0, tiled=True)
    moved = moved.reshape(NBLK, RING, 2, PART)
    theirs = lax.dynamic_slice_in_dim(moved, (1 - half) * 2, 2, axis=1)
    other = lax.ppermute(theirs, "rep", SWAP)
    return final(moved, other, amplitudes.shape)


def solution(mesh):
    fine = Mesh(mesh.devices.reshape(4, 8, 4, 2), ("y", "z", "x", "rep"))
    placed = (P(None, YZX, "rep", None), P(YZX, None, "rep", None), P())
    return jax.shard_map(
        on_device,
        mesh=fine,
        in_specs=placed,
        out_specs=P(None, YZX, "rep", None),
        check_vma=False,
    )
```

```python
import functools

import jax
import jax.numpy as jnp
from jax import lax
from jax.experimental import pallas as pl
from jax.experimental.pallas import tpu as pltpu
from jax.sharding import Mesh, PartitionSpec as P

NBLK = 8
YZX = ("y", "z", "x")
SWAP = [(0, 1), (1, 0)]
RING = 4
DEEP = 8
OWNERS = 32
LANES = 128
PART = 1024
STEP = 896
SPLIT_MIB = 56
VMEM = pl.BlockSpec(memory_space=pltpu.VMEM)
SMEM = pl.BlockSpec(memory_space=pltpu.SMEM)
ANY = pl.BlockSpec(memory_space=pl.ANY)


def shift(value, axis, by):
    n = lax.axis_size(axis)
    return lax.ppermute(value, axis, [(i, (i + by) % n) for i in range(n)])


def pick(value, index, axis=0):
    return lax.dynamic_index_in_dim(value, index, axis, keepdims=False)


def params(mib):
    return pltpu.CompilerParams(vmem_limit_bytes=mib << 20)


def cost(flops, nbytes):
    return pl.CostEstimate(flops=flops, bytes_accessed=nbytes, transcendentals=0)


def live_limit(count_ref):
    return count_ref[lax.axis_index("y") * 2 + lax.axis_index("z") // RING]


def prepare_kernel(amp_ref, out_hbm, piece_ref, sems):
    width = piece_ref.shape[3] // 2
    for g in range(NBLK):
        for k in range(RING):
            for r in range(2):
                piece_ref[g, k, :, r * width : (r + 1) * width] = amp_ref[g, r][
                    :, k * width : (k + 1) * width
                ]
    copies = [
        pltpu.make_async_copy(piece_ref, out_hbm.at[:, j], sems.at[j]) for j in range(RING)
    ]
    for copy in copies:
        copy.start()
    for copy in copies:
        copy.wait()


def prepare(amplitudes, width):
    return pl.pallas_call(
        prepare_kernel,
        in_specs=[VMEM],
        out_specs=ANY,
        out_shape=jax.ShapeDtypeStruct((NBLK, RING, RING, 1, 2 * width), jnp.float32),
        scratch_shapes=[
            pltpu.VMEM((NBLK, RING, 1, 2 * width), jnp.float32),
            pltpu.SemaphoreType.DMA((RING,)),
        ],
        cost_estimate=cost(0, 5 * 4 * amplitudes.size),
        compiler_params=params(56),
        name="prepare",
    )(amplitudes)


def split_kernel(count_ref, w_ref, *out_refs):
    half = lax.axis_index("rep")
    limit = live_limit(count_ref)
    base = (lax.axis_index("z") % RING) * w_ref.shape[1]
    for place, side in ((0, 1 - half), (1, half)):
        start = pl.multiple_of(side * STEP, LANES)
        high_ref, low_ref = out_refs[2 * place : 2 * place + 2]
        column = base + start + lax.broadcasted_iota(jnp.int32, (1, PART), 1)
        live = (column < limit).astype(jnp.float32)
        w = w_ref[:, pl.ds(start, PART)] * live
        high = w.astype(jnp.bfloat16)
        high_ref[...] = high
        low_ref[...] = (w - high.astype(jnp.float32)).astype(jnp.bfloat16)


def split_tile(pair_count, tile):
    depth, width = tile.shape
    rows = depth // 10
    return pl.pallas_call(
        split_kernel,
        grid=(10,),
        in_specs=[SMEM, pl.BlockSpec((rows, width), lambda i: (i, 0))],
        out_specs=[pl.BlockSpec((rows, PART), lambda i: (i, 0))] * 4,
        out_shape=[jax.ShapeDtypeStruct((depth, PART), jnp.bfloat16)] * 4,
        cost_estimate=cost(4 * depth * width, 8 * depth * width),
        compiler_params=params(SPLIT_MIB),
        name="split_tile",
    )(pair_count, tile)


def arrange_kernel(count_ref, got_ref, both_ref):
    width = got_ref.shape[3] // 2
    rows = both_ref.shape[0] // 2
    base = lax.axis_index("rep") * (RING * width) + lax.axis_index("x") * width
    slot = lax.broadcasted_iota(jnp.int32, (1, width), 1) + base
    live = (slot < live_limit(count_ref)).astype(jnp.float32)
    for x in range(RING):
        for r in range(2):
            a = got_ref[:, x, 0, r * width : (r + 1) * width] * live
            high = a.astype(jnp.bfloat16)
            at = (x * 2 + r) * OWNERS
            both_ref[at : at + OWNERS, :] = high
            both_ref[rows + at : rows + at + OWNERS, :] = (a - high.astype(jnp.float32)).astype(
                jnp.bfloat16
            )


def arrange(pair_count, got):
    width = got.shape[3] // 2
    rows = OWNERS * RING * 2
    return pl.pallas_call(
        arrange_kernel,
        in_specs=[SMEM, VMEM],
        out_specs=VMEM,
        out_shape=jax.ShapeDtypeStruct((2 * rows, width), jnp.bfloat16),
        cost_estimate=cost(0, 8 * rows * width),
        compiler_params=params(16),
        name="arrange",
    )(pair_count, got)


def contract(both, high, low):
    rows = both.shape[0] // 2
    dims = (((1,), (0,)), ((), ()))
    first = lax.dot_general(both, high, dims, preferred_element_type=jnp.float32)
    second = lax.dot_general(both[:rows], low, dims, preferred_element_type=jnp.float32)
    return first[:rows] + (first[rows:] + second)


def gather_kernel(own_ref, left_a, right_a, left_b, right_b, out_ref):
    out_ref[:, 0, :] = own_ref[:OWNERS] + (left_a[...] + right_a[...])
    out_ref[:, 1, :] = own_ref[OWNERS:] + (left_b[...] + right_b[...])


def gather(parts):
    return pl.pallas_call(
        gather_kernel,
        in_specs=[VMEM] * len(parts),
        out_specs=VMEM,
        out_shape=jax.ShapeDtypeStruct((OWNERS, 2, PART), jnp.float32),
        compiler_params=params(16),
        cost_estimate=cost(0, 4 * 4 * OWNERS * 2 * PART),
        name="gather_rows",
    )(*parts)


def final_kernel(moved_ref, other_ref, out_ref):
    def write(low_of, high_of):
        for g in range(NBLK):
            for r in range(2):
                for j in range(2):
                    base = j * (PART + STEP)
                    out_ref[g, r, :, base : base + PART] = low_of(g, j, r)
                    out_ref[g, r, :, base + PART : base + PART + STEP] = high_of(g, j, r)[:, LANES:]

    half = lax.axis_index("rep")

    @pl.when(half == 0)
    def _():
        write(
            lambda g, j, r: moved_ref[g, j, r : r + 1, :],
            lambda g, j, r: other_ref[g, j, r : r + 1, :],
        )

    @pl.when(half == 1)
    def _():
        write(
            lambda g, j, r: other_ref[g, j, r : r + 1, :],
            lambda g, j, r: moved_ref[g, 2 + j, r : r + 1, :],
        )


def final(moved, other, shape):
    return pl.pallas_call(
        final_kernel,
        in_specs=[VMEM, VMEM],
        out_specs=VMEM,
        out_shape=jax.ShapeDtypeStruct(shape, jnp.float32),
        compiler_params=params(16),
        name="final_rows",
    )(moved, other)


def on_device(amplitudes, integrals, pair_count):
    kc_width = integrals.shape[3]
    half = lax.axis_index("rep")
    my_x = lax.axis_index("x")
    outgoing = prepare(amplitudes, kc_width).reshape(-1, 1, 2 * kc_width)
    got = lax.all_to_all(outgoing, YZX, split_axis=0, concat_axis=0, tiled=True)
    split = split_tile(pair_count, integrals[0, :, 0, :].T)
    got, split = lax.optimization_barrier((got, split))
    both = arrange(pair_count, got.reshape(OWNERS, RING, 1, 2 * kc_width))
    arrived = lax.ppermute(contract(both, split[0], split[1]), "rep", SWAP)
    pair_sum = contract(both, split[2], split[3]) + arrived
    pair_sum = pair_sum.reshape(RING, 2, OWNERS, PART)
    ours, right, across, left = [pick(pair_sum, (my_x + s) % RING) for s in range(RING)]
    by_right = shift(across[0], "x", 1)
    by_left = shift(across[1], "x", -1)
    right_b = shift(right[1], "x", 1)
    left_a = shift(left[0], "x", -1)
    right_a = shift(right[0] + by_right, "x", 1)
    left_b = shift(left[1] + by_left, "x", -1)
    leaving = gather([ours.reshape(2 * OWNERS, PART), left_a, right_a, left_b, right_b])
    moved = lax.all_to_all(leaving, ("y", "z"), split_axis=0, concat_axis=0, tiled=True)
    moved = moved.reshape(NBLK, RING, 2, PART)
    theirs = lax.dynamic_slice_in_dim(moved, (1 - half) * 2, 2, axis=1)
    other = lax.ppermute(theirs, "rep", SWAP)
    return final(moved, other, amplitudes.shape)


def solution(mesh):
    fine = Mesh(mesh.devices.reshape(4, 8, 4, 2), ("y", "z", "x", "rep"))
    placed = (P(None, YZX, "rep", None), P(YZX, None, "rep", None), P())
    return jax.shard_map(
        on_device,
        mesh=fine,
        in_specs=placed,
        out_specs=P(None, YZX, "rep", None),
        check_vma=False,
    )
```

```python
import functools

import jax
import jax.numpy as jnp
from jax import lax
from jax.experimental import pallas as pl
from jax.experimental.pallas import tpu as pltpu
from jax.sharding import Mesh, PartitionSpec as P

NBLK = 8
YZX = ("y", "z", "x")
SWAP = [(0, 1), (1, 0)]
RING = 4
DEEP = 8
OWNERS = 32
LANES = 128
PART = 1024
STEP = 896
SPLIT_MIB = 56
PARTS = 2
VMEM = pl.BlockSpec(memory_space=pltpu.VMEM)
SMEM = pl.BlockSpec(memory_space=pltpu.SMEM)
ANY = pl.BlockSpec(memory_space=pl.ANY)


def shift(value, axis, by):
    n = lax.axis_size(axis)
    return lax.ppermute(value, axis, [(i, (i + by) % n) for i in range(n)])


def pick(value, index, axis=0):
    return lax.dynamic_index_in_dim(value, index, axis, keepdims=False)


def params(mib):
    return pltpu.CompilerParams(vmem_limit_bytes=mib << 20)


def cost(flops, nbytes):
    return pl.CostEstimate(flops=flops, bytes_accessed=nbytes, transcendentals=0)


def live_limit(count_ref):
    return count_ref[lax.axis_index("y") * 2 + lax.axis_index("z") // RING]


def prepare_kernel(amp_ref, out_hbm, piece_ref, sems):
    step = pl.program_id(0)
    count = amp_ref.shape[0]
    width = piece_ref.shape[3] // 2

    def copies(part):
        blocks = pl.ds(part * count, count)
        return [
            pltpu.make_async_copy(piece_ref.at[blocks], out_hbm.at[blocks, j], sems.at[part, j])
            for j in range(RING)
        ]

    for g in range(count):
        for k in range(RING):
            for r in range(2):
                piece_ref[step * count + g, k, :, r * width : (r + 1) * width] = amp_ref[g, r][
                    :, k * width : (k + 1) * width
                ]
    for copy in copies(step):
        copy.start()

    @pl.when(step == PARTS - 1)
    def _():
        for part in range(PARTS):
            for copy in copies(part):
                copy.wait()


def prepare(amplitudes, width):
    count = NBLK // PARTS
    return pl.pallas_call(
        prepare_kernel,
        grid=(PARTS,),
        in_specs=[pl.BlockSpec((count,) + amplitudes.shape[1:], lambda i: (i, 0, 0, 0))],
        out_specs=ANY,
        out_shape=jax.ShapeDtypeStruct((NBLK, RING, RING, 1, 2 * width), jnp.float32),
        scratch_shapes=[
            pltpu.VMEM((NBLK, RING, 1, 2 * width), jnp.float32),
            pltpu.SemaphoreType.DMA((PARTS, RING)),
        ],
        cost_estimate=cost(0, 5 * 4 * amplitudes.size),
        compiler_params=params(56),
        name="prepare",
    )(amplitudes)


def split_kernel(count_ref, w_ref, *out_refs):
    half = lax.axis_index("rep")
    limit = live_limit(count_ref)
    base = (lax.axis_index("z") % RING) * w_ref.shape[1]
    for place, side in ((0, 1 - half), (1, half)):
        start = pl.multiple_of(side * STEP, LANES)
        high_ref, low_ref = out_refs[2 * place : 2 * place + 2]
        column = base + start + lax.broadcasted_iota(jnp.int32, (1, PART), 1)
        live = (column < limit).astype(jnp.float32)
        w = w_ref[:, pl.ds(start, PART)] * live
        high = w.astype(jnp.bfloat16)
        high_ref[...] = high
        low_ref[...] = (w - high.astype(jnp.float32)).astype(jnp.bfloat16)


def split_tile(pair_count, tile):
    depth, width = tile.shape
    rows = depth // 10
    return pl.pallas_call(
        split_kernel,
        grid=(10,),
        in_specs=[SMEM, pl.BlockSpec((rows, width), lambda i: (i, 0))],
        out_specs=[pl.BlockSpec((rows, PART), lambda i: (i, 0))] * 4,
        out_shape=[jax.ShapeDtypeStruct((depth, PART), jnp.bfloat16)] * 4,
        cost_estimate=cost(4 * depth * width, 8 * depth * width),
        compiler_params=params(SPLIT_MIB),
        name="split_tile",
    )(pair_count, tile)


def arrange_kernel(count_ref, got_ref, both_ref):
    width = got_ref.shape[3] // 2
    rows = both_ref.shape[0] // 2
    base = lax.axis_index("rep") * (RING * width) + lax.axis_index("x") * width
    slot = lax.broadcasted_iota(jnp.int32, (1, width), 1) + base
    live = (slot < live_limit(count_ref)).astype(jnp.float32)
    for x in range(RING):
        for r in range(2):
            a = got_ref[:, x, 0, r * width : (r + 1) * width] * live
            high = a.astype(jnp.bfloat16)
            at = (x * 2 + r) * OWNERS
            both_ref[at : at + OWNERS, :] = high
            both_ref[rows + at : rows + at + OWNERS, :] = (a - high.astype(jnp.float32)).astype(
                jnp.bfloat16
            )


def arrange(pair_count, got):
    width = got.shape[3] // 2
    rows = OWNERS * RING * 2
    return pl.pallas_call(
        arrange_kernel,
        in_specs=[SMEM, VMEM],
        out_specs=VMEM,
        out_shape=jax.ShapeDtypeStruct((2 * rows, width), jnp.bfloat16),
        cost_estimate=cost(0, 8 * rows * width),
        compiler_params=params(16),
        name="arrange",
    )(pair_count, got)


def contract(both, high, low):
    rows = both.shape[0] // 2
    dims = (((1,), (0,)), ((), ()))
    first = lax.dot_general(both, high, dims, preferred_element_type=jnp.float32)
    second = lax.dot_general(both[:rows], low, dims, preferred_element_type=jnp.float32)
    return first[:rows] + (first[rows:] + second)


def gather_kernel(own_ref, left_a, right_a, left_b, right_b, out_ref):
    out_ref[:, 0, :] = own_ref[:OWNERS] + (left_a[...] + right_a[...])
    out_ref[:, 1, :] = own_ref[OWNERS:] + (left_b[...] + right_b[...])


def gather(parts):
    return pl.pallas_call(
        gather_kernel,
        in_specs=[VMEM] * len(parts),
        out_specs=VMEM,
        out_shape=jax.ShapeDtypeStruct((OWNERS, 2, PART), jnp.float32),
        compiler_params=params(16),
        cost_estimate=cost(0, 4 * 4 * OWNERS * 2 * PART),
        name="gather_rows",
    )(*parts)


def final_kernel(moved_ref, other_ref, out_ref):
    def write(low_of, high_of):
        for g in range(NBLK):
            for r in range(2):
                for j in range(2):
                    base = j * (PART + STEP)
                    out_ref[g, r, :, base : base + PART] = low_of(g, j, r)
                    out_ref[g, r, :, base + PART : base + PART + STEP] = high_of(g, j, r)[:, LANES:]

    half = lax.axis_index("rep")

    @pl.when(half == 0)
    def _():
        write(
            lambda g, j, r: moved_ref[g, j, r : r + 1, :],
            lambda g, j, r: other_ref[g, j, r : r + 1, :],
        )

    @pl.when(half == 1)
    def _():
        write(
            lambda g, j, r: other_ref[g, j, r : r + 1, :],
            lambda g, j, r: moved_ref[g, 2 + j, r : r + 1, :],
        )


def final(moved, other, shape):
    return pl.pallas_call(
        final_kernel,
        in_specs=[VMEM, VMEM],
        out_specs=VMEM,
        out_shape=jax.ShapeDtypeStruct(shape, jnp.float32),
        compiler_params=params(16),
        name="final_rows",
    )(moved, other)


def on_device(amplitudes, integrals, pair_count):
    kc_width = integrals.shape[3]
    half = lax.axis_index("rep")
    my_x = lax.axis_index("x")
    outgoing = prepare(amplitudes, kc_width).reshape(-1, 1, 2 * kc_width)
    got = lax.all_to_all(outgoing, YZX, split_axis=0, concat_axis=0, tiled=True)
    split = split_tile(pair_count, integrals[0, :, 0, :].T)
    got, split = lax.optimization_barrier((got, split))
    both = arrange(pair_count, got.reshape(OWNERS, RING, 1, 2 * kc_width))
    arrived = lax.ppermute(contract(both, split[0], split[1]), "rep", SWAP)
    pair_sum = contract(both, split[2], split[3]) + arrived
    pair_sum = pair_sum.reshape(RING, 2, OWNERS, PART)
    ours, right, across, left = [pick(pair_sum, (my_x + s) % RING) for s in range(RING)]
    by_right = shift(across[0], "x", 1)
    by_left = shift(across[1], "x", -1)
    right_b = shift(right[1], "x", 1)
    left_a = shift(left[0], "x", -1)
    right_a = shift(right[0] + by_right, "x", 1)
    left_b = shift(left[1] + by_left, "x", -1)
    leaving = gather([ours.reshape(2 * OWNERS, PART), left_a, right_a, left_b, right_b])
    moved = lax.all_to_all(leaving, ("y", "z"), split_axis=0, concat_axis=0, tiled=True)
    moved = moved.reshape(NBLK, RING, 2, PART)
    theirs = lax.dynamic_slice_in_dim(moved, (1 - half) * 2, 2, axis=1)
    other = lax.ppermute(theirs, "rep", SWAP)
    return final(moved, other, amplitudes.shape)


def solution(mesh):
    fine = Mesh(mesh.devices.reshape(4, 8, 4, 2), ("y", "z", "x", "rep"))
    placed = (P(None, YZX, "rep", None), P(YZX, None, "rep", None), P())
    return jax.shard_map(
        on_device,
        mesh=fine,
        in_specs=placed,
        out_specs=P(None, YZX, "rep", None),
        check_vma=False,
    )
```
